32 devices in a mesh: gx: 8 (over z, core), gy: 4 (over y, x).
Axes of the slice: x: 2, y: 2, z: 4, core: 2. Of those that a mesh axis runs over, the one named last changes fastest.
Arguments:
- iti: float32 [8, 4, 2, 512, 512], P('gx', 'gy'), may hold values from -3 to 3
- side: int32 [8, 4], P('gx', 'gy'), may hold values from 0 to 1, as said below
- owner: int32 [8, 4, 4], P('gx', 'gy'), may hold values from 0 to 3, each once within a row
Outputs:
- panels: float32 [8, 4, 2, 4, 96, 768], P('gx', 'gy')
The draws below stay inside these ranges and needn't reach their ends.
Inputs may be any that keep to these rules, and one draw needn't show every extreme that they name: `side`: boxes (i, j) and (i + 4, j) are the two siblings of one parent and have different sides. `owner`: for each box the owners of its panels are all different.
All inputs are finite; a program needn't handle non-finite values.
Results may differ from the reference program's by a relative error of at most 0.0003.
Values sent between devices are 32-bit elements; how exact they have to be, the bound alone decides.
No kernel may reach another device: no remote copies, remote signals or barrier semaphores. Data moves between devices by JAX's collectives and lax.ppermute only.
A program may use at most 64 MiB of HBM per device.

```python
import math
import jax
import jax.numpy as jnp
from jax import lax

E = 128
SWEEPS = 15
BOX_COLS = 8
BOX_ROWS = 4
HALF_GX = 4
PANEL = 96


def draw_iti(key, part):
    shape = (BOX_COLS, BOX_ROWS, 2, 4 * E, 4 * E)
    spread = 0.665 / E ** 0.5
    values = jnp.clip(jax.random.normal(key, shape, jnp.float32) * spread, -4.0 * spread, 4.0 * spread)
    return values.astype(jnp.float32)


def draw_side(key, part):
    halves = jax.random.randint(key, (HALF_GX, BOX_ROWS), 0, 2, jnp.int32)
    return jnp.concatenate([halves, 1 - halves], axis=0).astype(jnp.int32)


def setup_inputs(seed: int = 0) -> dict:
    key_list = jax.random.split(jax.random.key(seed), 4)
    iti = draw_iti(jax.random.fold_in(key_list[3], 71), 0)
    side = draw_side(jax.random.fold_in(key_list[3], 71), 0)
    owner = jax.vmap(lambda own: jax.random.permutation(own, BOX_ROWS))(jax.random.split(key_list[2], BOX_COLS * BOX_ROWS)).reshape((BOX_COLS, BOX_ROWS, BOX_ROWS)).astype(jnp.int32)
    return dict(iti=iti, side=side, owner=owner)


def cprod(left, right):
    hp = lax.Precision.HIGHEST
    rr = jnp.dot(left[0], right[0], precision=hp, preferred_element_type=jnp.float32)
    ii = jnp.dot(left[1], right[1], precision=hp, preferred_element_type=jnp.float32)
    ri = jnp.dot(left[0], right[1], precision=hp, preferred_element_type=jnp.float32)
    ir = jnp.dot(left[1], right[0], precision=hp, preferred_element_type=jnp.float32)
    return jnp.stack([rr - ii, ri + ir])

def merge_one(ownmap, partner, east):
    ext = 3 * E
    p_ss = partner[:, :, ext:]
    p_se = partner[:, :, :ext]
    interface = cprod(p_ss, ownmap[:, ext:, ext:])
    own_cols = cprod(p_ss, ownmap[:, ext:, :ext])
    flag = east == 1
    start = jnp.where(flag, jnp.concatenate([p_se, own_cols], axis=-1), jnp.concatenate([own_cols, p_se], axis=-1))
    exterior = ownmap[:, :ext, :ext]
    zero = jnp.zeros_like(exterior)
    base = jnp.where(flag, jnp.concatenate([zero, exterior], axis=-1), jnp.concatenate([exterior, zero], axis=-1))
    total = start
    power = interface
    levels = (SWEEPS + 1).bit_length() - 1
    for level in range(levels):
        total = total + cprod(power, total)
        if level + 1 < levels:
            power = cprod(power, power)
    merged = (base + cprod(ownmap[:, :ext, ext:], total)) * math.sqrt(E)
    return merged

def reference(iti, side, owner):
    count = BOX_COLS * BOX_ROWS
    partner = jnp.roll(iti, HALF_GX, axis=0)[:, :, :, 3 * E:, :]
    merged = lax.map(lambda item: merge_one(item[0], item[1], item[2]), (iti.reshape(count, 2, 4 * E, 4 * E), partner.reshape(count, 2, E, 4 * E), side.reshape(count)))
    merged = merged.reshape(BOX_COLS, BOX_ROWS, 2, BOX_ROWS, PANEL, 6 * E)
    places = jnp.arange(BOX_ROWS, dtype=jnp.int32)
    match = (owner[:, :, :, None] == places[None, None, None, :]).astype(jnp.int32)
    inverse = lax.optimization_barrier(jnp.sum(places[None, None, :, None] * match, axis=2)).astype(jnp.int32)
    gathered = jnp.take_along_axis(merged, inverse[:, :, None, :, None, None], axis=3)
    return jnp.transpose(gathered, (0, 3, 2, 1, 4, 5))
```

```python
import functools
import math

import jax
import jax.numpy as jnp
from jax import lax
from jax.experimental import pallas as pl
from jax.experimental.pallas import tpu as pltpu
from jax.sharding import PartitionSpec as P

SWEEPS = 15
VMEM = pl.BlockSpec(memory_space=pltpu.VMEM)
SMEM = pl.BlockSpec(memory_space=pltpu.SMEM)
ANY = pl.BlockSpec(memory_space=pl.ANY)


def limit(mib):
    return pltpu.CompilerParams(vmem_limit_bytes=mib << 20)


def permute(x, axis, offset):
    return lax.ppermute(x, axis, [(i, i ^ offset) for i in range(lax.axis_size(axis))])


def halves(x):
    high = x.astype(jnp.bfloat16)
    return high, (x - high.astype(jnp.float32)).astype(jnp.bfloat16)


def matmul(left, right):
    dot = functools.partial(jnp.dot, preferred_element_type=jnp.float32)
    return dot(left[0], right[0]) + (dot(left[1], right[0]) + dot(left[0], right[1]))


def rows_of(ref, rows, cols):
    return jnp.concatenate([ref[0, rows, cols], ref[1, rows, cols]], axis=1)


def embed(x):
    half = x.shape[1] // 2
    real, imag = x[:, :half], x[:, half:]
    return halves(jnp.concatenate([x, jnp.concatenate([-imag, real], axis=1)], axis=0))


def panel_of(owner_ref, dest, groups):
    index = jnp.int32(0)
    for p in range(groups):
        index = jnp.where(owner_ref[p] == dest, jnp.int32(p), index)
    return index


def own_half_kernel(edge, ext, groups, owner_ref, iti_ref, qss_ref, high_ref, low_ref, *out_refs):
    rows_each = ext // groups
    me = lax.axis_index("gy")
    starts = [pl.multiple_of(panel_of(owner_ref, me ^ k, groups) * rows_each, 8) for k in range(groups)]
    weight = math.sqrt(edge)
    shared = slice(ext, ext + edge)
    rss = embed(rows_of(iti_ref, shared, shared))
    qss = halves(rows_of(qss_ref, slice(None), slice(None)))
    power = matmul(qss, rss)
    total = jnp.concatenate([rows_of(iti_ref, pl.ds(s, rows_each), shared) for s in starts], axis=0)
    rse = embed(rows_of(iti_ref, shared, slice(0, ext)))
    own_cols = embed(matmul(qss, rse))
    levels = (SWEEPS + 1).bit_length() - 1
    for level in range(levels):
        right = embed(power)
        if level + 1 < levels:
            power = matmul(halves(power), right)
        total = total + matmul(halves(total), right)
    total = halves(total)
    high_ref[...] = total[0]
    low_ref[...] = total[1]
    half = matmul(total, own_cols)
    for k in range(groups):
        for c in range(2):
            block = half[k * rows_each : (k + 1) * rows_each, c * ext : (c + 1) * ext]
            out_refs[k][c] = (iti_ref[c, pl.ds(starts[k], rows_each), 0:ext] + block) * weight


def other_half_kernel(edge, groups, high_ref, low_ref, qse_ref, *out_refs):
    rows_each = high_ref.shape[0] // groups
    weight = math.sqrt(edge)
    cols = qse_ref.shape[-1]
    half = matmul((high_ref[...], low_ref[...]), embed(rows_of(qse_ref, slice(None), slice(None))))
    for k in range(groups):
        for c in range(2):
            out_refs[k][c] = half[k * rows_each : (k + 1) * rows_each, c * cols : (c + 1) * cols] * weight


def store_kernel(groups, ext, first, side_refs, block_refs, out_ref, sems):
    me = lax.axis_index("gy")
    copies = []
    for k in range(groups):
        side = (side_refs[k][0] == 1).astype(jnp.int32)
        own = side * ext
        col = pl.multiple_of(own if first is None else (ext - own) + first, 128)
        rows, cols = block_refs[k].shape[1:]
        for c in range(2):
            copy = pltpu.make_async_copy(
                block_refs[k].at[c], out_ref.at[c, me ^ k, :, pl.ds(col, cols)], sems.at[k, c]
            )
            copy.start()
            copies.append(copy)
    for copy in copies:
        copy.wait()


def store(sides, blocks, first, ext, out=None):
    groups = len(blocks)
    rows = blocks[0].shape[1]
    shape = jax.ShapeDtypeStruct((2, groups, rows, 2 * ext), jnp.float32)

    def kernel(*refs):
        out_ref, sems = refs[-2:]
        store_kernel(groups, ext, first, refs[:groups], refs[groups : 2 * groups], out_ref, sems)

    args = [*sides, *blocks] + ([] if out is None else [out])
    return pl.pallas_call(
        kernel,
        out_shape=shape,
        in_specs=[SMEM] * groups + [VMEM] * groups + ([] if out is None else [ANY]),
        out_specs=ANY,
        compiler_params=limit(4),
        scratch_shapes=[pltpu.SemaphoreType.DMA((groups, 2))],
        input_output_aliases={} if out is None else {2 * groups: 0},
    )(*args)


def on_device(iti, side, owner):
    ownmap = iti[0, 0]
    edge = ownmap.shape[-1] // 4
    ext = 3 * edge
    groups = lax.axis_size("gy")
    rows_each = ext // groups
    across = lax.axis_size("gx") // 2
    mine = side[0]
    sides = [mine] + [permute(mine, "gy", k) for k in range(1, groups)]
    qss = permute(ownmap[:, ext:, ext:], "gx", across)
    cuts = [(0, 2 * edge), (2 * edge, ext)]
    qse = []
    gate = qss
    for lo, hi in cuts:
        part, gate = lax.optimization_barrier((ownmap[:, ext:, lo:hi], gate))
        gate = permute(part, "gx", across)
        qse.append(gate)
    panel = jax.ShapeDtypeStruct((2, rows_each, ext), jnp.float32)
    factor = jax.ShapeDtypeStruct((ext, 2 * edge), jnp.bfloat16)
    high, low, *blocks = pl.pallas_call(
        functools.partial(own_half_kernel, edge, ext, groups),
        out_shape=[factor, factor] + [panel] * groups,
        in_specs=[SMEM, VMEM, VMEM],
        out_specs=[VMEM] * (2 + groups),
        compiler_params=limit(24),
    )(owner[0, 0], ownmap, qss)
    blocks = [blocks[0]] + [permute(blocks[k], "gy", k) for k in range(1, groups)]
    out = store(sides, blocks, None, ext)
    for (lo, hi), part in zip(cuts, qse):
        panel = jax.ShapeDtypeStruct((2, rows_each, hi - lo), jnp.float32)
        blocks = pl.pallas_call(
            functools.partial(other_half_kernel, edge, groups),
            out_shape=[panel] * groups,
            in_specs=[VMEM] * 3,
            out_specs=[VMEM] * groups,
            compiler_params=limit(16),
        )(high, low, part)
        blocks = [blocks[0]] + [permute(blocks[k], "gy", k) for k in range(1, groups)]
        out = store(sides, blocks, lo, ext, out)
    return out[None, None]


def solution(mesh):
    in_specs = (P("gx", "gy", None, None, None), P("gx", "gy"), P("gx", "gy", None))
    out_specs = P("gx", "gy", None, None, None, None)
    return jax.shard_map(
        on_device, mesh=mesh, in_specs=in_specs, out_specs=out_specs, check_vma=False
    )
```

```python
import functools
import math

import jax
import jax.numpy as jnp
from jax import lax
from jax.experimental import pallas as pl
from jax.experimental.pallas import tpu as pltpu
from jax.sharding import PartitionSpec as P


SWEEPS = 15
LEVELS = (SWEEPS + 1).bit_length() - 1
PIECES = 2
VMEM = pl.BlockSpec(memory_space=pltpu.VMEM)
SMEM = pl.BlockSpec(memory_space=pltpu.SMEM)
HBM = pl.BlockSpec(memory_space=pltpu.MemorySpace.HBM)


def limit(mib):
    return pltpu.CompilerParams(vmem_limit_bytes=mib << 20)


def f32(*shape):
    return jax.ShapeDtypeStruct(shape, jnp.float32)


def bf16(*shape):
    return jax.ShapeDtypeStruct(shape, jnp.bfloat16)


def permute(x, axis, offset):
    return lax.ppermute(x, axis, [(i, i ^ offset) for i in range(lax.axis_size(axis))])


def exchange(blocks):
    received = [blocks[0]]
    for k in range(1, len(blocks)):
        received.append(permute(blocks[k], "gy", k))
    return received


def call(kernel, **options):
    def run(*args):
        return pl.pallas_call(kernel, **options)(*args)

    return run


def halves(x):
    high = x.astype(jnp.bfloat16)
    return high, (x - high.astype(jnp.float32)).astype(jnp.bfloat16)


def matmul(left, right):
    dot = functools.partial(jnp.dot, preferred_element_type=jnp.float32)
    return dot(left[0], right[0]) + (dot(left[1], right[0]) + dot(left[0], right[1]))


def embed(real, imag):
    top = jnp.concatenate([real, imag], axis=1)
    return halves(jnp.concatenate([top, jnp.concatenate([-imag, real], axis=1)], axis=0))


def split_embed(x):
    half = x.shape[1] // 2
    return embed(x[:, :half], x[:, half:])


def panel_of(owner_ref, dest, groups):
    index = jnp.int32(0)
    for p in range(groups):
        index = jnp.where(owner_ref[p] == dest, jnp.int32(p), index)
    return index


def prepare_kernel(edge, ext, groups, cuts, owner_ref, iti_ref, *refs):
    parts, refs = refs[: len(cuts)], refs[len(cuts) :]
    base_ref, res_ref, res_high, res_low, rss_high, rss_low, rse_high, rse_low, shared_ref, sems = refs
    rows_each = ext // groups
    me = lax.axis_index("gy")
    pending = []

    def fetch(src, dst):
        copy = pltpu.make_async_copy(src, dst, sems.at[len(pending)])
        copy.start()
        pending.append(1)
        return copy

    shared = fetch(iti_ref.at[:, ext:, :], shared_ref)
    blocks, others = [], []
    for k in range(groups):
        start = pl.multiple_of(panel_of(owner_ref, me ^ k, groups) * rows_each, 8)
        rows = pl.ds(k * rows_each, rows_each)
        for c in range(2):
            blocks.append(fetch(iti_ref.at[c, pl.ds(start, rows_each), ext:], res_ref.at[rows, c * edge : (c + 1) * edge]))
            others.append(fetch(iti_ref.at[c, pl.ds(start, rows_each), :ext], base_ref.at[c, rows, :]))
    for (lo, hi), part in zip(cuts, parts):
        others.append(fetch(iti_ref.at[:, ext:, lo:hi], part))
    shared.wait()
    rss_high[...], rss_low[...] = embed(shared_ref[0, :, ext:], shared_ref[1, :, ext:])
    rse_high[...], rse_low[...] = embed(shared_ref[0, :, :ext], shared_ref[1, :, :ext])
    for copy in blocks:
        copy.wait()
    res_high[...], res_low[...] = halves(res_ref[...])
    for copy in others:
        copy.wait()


def factor_kernel(edge, ext, rows, qss_ref, base_ref, res_ref, res_high, res_low, rss_high, rss_low, rse_high, rse_low, *refs):
    pow_high, pow_low, cols_high, cols_low, far_high, far_low, out_ref = refs
    qss = halves(jnp.concatenate([qss_ref[0], qss_ref[1]], axis=1))
    power = matmul(qss, (rss_high[...], rss_low[...]))
    total = res_ref[ext - rows :]
    left = res_high[ext - rows :], res_low[ext - rows :]
    for level in range(LEVELS):
        right = split_embed(power)
        pow_high[level], pow_low[level] = right
        if level + 1 < LEVELS:
            both = matmul([jnp.concatenate(pair, axis=0) for pair in zip(halves(power), left)], right)
            power = both[:edge]
            total = total + both[edge:]
        else:
            total = total + matmul(left, right)
        left = halves(total)
    far_high[...], far_low[...] = left
    cols = split_embed(matmul(qss, (rse_high[...], rse_low[...])))
    cols_high[...], cols_low[...] = cols
    finish(edge, ext, [out_ref], matmul(left, cols), base_ref, ext - rows)


def finish(edge, ext, out_refs, half, base_ref, start):
    weight = math.sqrt(edge)
    rows = half.shape[0] // len(out_refs)
    for n, out_ref in enumerate(out_refs):
        for c in range(2):
            block = half[n * rows : (n + 1) * rows, c * ext : (c + 1) * ext]
            out_ref[c] = (base_ref[c, start + n * rows : start + (n + 1) * rows, :] + block) * weight


def own_half_kernel(edge, ext, rows, base_ref, res_ref, res_high, res_low, pow_high, pow_low, cols_high, cols_low, *refs):
    high_ref, low_ref, *out_refs = refs
    total = res_ref[: ext - rows]
    left = res_high[: ext - rows], res_low[: ext - rows]
    for level in range(LEVELS):
        total = total + matmul(left, (pow_high[level], pow_low[level]))
        left = halves(total)
    high_ref[...], low_ref[...] = left
    if out_refs:
        finish(edge, ext, out_refs, matmul([x[rows:] for x in left], (cols_high[...], cols_low[...])), base_ref, rows)


def mine_kernel(edge, ext, rows, base_ref, high_ref, low_ref, cols_high, cols_low, out_ref):
    half = matmul((high_ref[:rows], low_ref[:rows]), (cols_high[...], cols_low[...]))
    finish(edge, ext, [out_ref], half, base_ref, 0)


def other_half_kernel(edge, groups, high_ref, low_ref, far_high, far_low, qse_ref, *out_refs):
    weight = math.sqrt(edge)
    rows = far_high.shape[0]
    cols = qse_ref.shape[-1]
    left = [jnp.concatenate([a[...], b[...]], axis=0) for a, b in ((high_ref, far_high), (low_ref, far_low))]
    half = matmul(left, embed(qse_ref[0], qse_ref[1]))
    for k in range(groups):
        for c in range(2):
            out_refs[k][c] = half[k * rows : (k + 1) * rows, c * cols : (c + 1) * cols] * weight


def store(sides, parts, ext, out=None):
    groups = len(sides)
    count = groups * len(parts)
    rows = parts[0][1][0].shape[1]

    def kernel(*refs):
        out_ref, sems = refs[-2:]
        me = lax.axis_index("gy")
        copies = []
        for k in range(groups):
            own = (jnp.max(refs[k][...]) > 0.5).astype(jnp.int32) * ext
            for n, (first, _) in enumerate(parts):
                block = refs[groups + n * groups + k]
                col = pl.multiple_of(own if first is None else ext - own + first, 128)
                for c in range(2):
                    dst = out_ref.at[c, me ^ k, :, pl.ds(col, block.shape[-1])]
                    copy = pltpu.make_async_copy(block.at[c], dst, sems.at[2 * (n * groups + k) + c])
                    copy.start()
                    copies.append(copy)
        for copy in copies:
            copy.wait()

    args = [*sides, *(b for _, blocks in parts for b in blocks)] + ([] if out is None else [out])
    return call(
        kernel,
        out_shape=f32(2, groups, rows, 2 * ext),
        in_specs=[VMEM] * (groups + count) + ([] if out is None else [HBM]),
        out_specs=HBM,
        scratch_shapes=[pltpu.SemaphoreType.DMA((2 * count,))],
        input_output_aliases={} if out is None else {groups + count: 0},
        compiler_params=limit(4),
    )(*args)


def on_device(iti, side, owner):
    ownmap = iti[0, 0]
    edge = ownmap.shape[-1] // 4
    ext = 3 * edge
    groups = lax.axis_size("gy")
    rows_each = ext // groups
    across = lax.axis_size("gx") // 2
    cuts = [(0 * edge, 2 * edge), (2 * edge, 3 * edge)]
    assert len(cuts) == PIECES
    qss = permute(ownmap[:, ext:, ext:], "gx", across)
    *pieces, base, res, res_high, res_low, rss_high, rss_low, rse_high, rse_low = call(
        functools.partial(prepare_kernel, edge, ext, groups, cuts),
        out_shape=[f32(2, edge, hi - lo) for lo, hi in cuts]
        + [f32(2, ext, ext), f32(ext, 2 * edge), bf16(ext, 2 * edge), bf16(ext, 2 * edge)]
        + [bf16(2 * edge, 2 * edge)] * 2
        + [bf16(2 * edge, 2 * ext)] * 2,
        in_specs=[SMEM, HBM],
        out_specs=[VMEM] * (8 + len(cuts)),
        scratch_shapes=[pltpu.VMEM((2, edge, 4 * edge), jnp.float32), pltpu.SemaphoreType.DMA((1 + 4 * groups + len(cuts),))],
        compiler_params=limit(12),
    )(owner[0, 0], ownmap)
    pow_high, pow_low, cols_high, cols_low, far_high, far_low, farthest = call(
        functools.partial(factor_kernel, edge, ext, rows_each),
        out_shape=[bf16(LEVELS, 2 * edge, 2 * edge)] * 2
        + [bf16(2 * edge, 2 * ext)] * 2
        + [bf16(rows_each, 2 * edge)] * 2
        + [f32(2, rows_each, ext)],
        in_specs=[VMEM] * 9,
        out_specs=[VMEM] * 7,
        compiler_params=limit(16),
    )(qss, base, res, res_high, res_low, rss_high, rss_low, rse_high, rse_low)
    qse = []
    for piece in pieces:
        if qse:
            piece, qse[-1] = lax.optimization_barrier((piece, qse[-1]))
        else:
            piece, far_high = lax.optimization_barrier((piece, far_high))
        qse.append(permute(piece, "gx", across))
    high, low, *own = call(
        functools.partial(own_half_kernel, edge, ext, rows_each),
        out_shape=[bf16(ext - rows_each, 2 * edge)] * 2 + [f32(2, rows_each, ext)] * (groups - 2),
        in_specs=[VMEM] * 8,
        out_specs=[VMEM] * groups,
        compiler_params=limit(16),
    )(base, res, res_high, res_low, pow_high, pow_low, cols_high, cols_low)
    mine = call(
        functools.partial(mine_kernel, edge, ext, rows_each),
        out_shape=f32(2, rows_each, ext),
        in_specs=[VMEM] * 5,
        out_specs=VMEM,
        compiler_params=limit(16),
    )(base, high, low, cols_high, cols_low)
    own = [mine, *own, farthest]
    own = exchange(own)
    flag = jnp.full((8, 128), side[0, 0].astype(jnp.float32))
    flag, high = lax.optimization_barrier((flag, high))
    sides = exchange([flag] * groups)
    parts = []
    for (lo, hi), part in zip(cuts, qse):
        blocks = call(
            functools.partial(other_half_kernel, edge, groups),
            out_shape=[f32(2, rows_each, hi - lo)] * groups,
            in_specs=[VMEM] * 5,
            out_specs=[VMEM] * groups,
            compiler_params=limit(12),
        )(high, low, far_high, far_low, part)
        parts.append((lo, exchange(blocks)))
    out = store(sides, [(None, own), *parts[:-1]], ext)
    out = store(sides, parts[-1:], ext, out)
    return out[None, None]


def solution(mesh):
    in_specs = (P("gx", "gy", None, None, None), P("gx", "gy"), P("gx", "gy", None))
    out_specs = P("gx", "gy", None, None, None, None)
    return jax.shard_map(on_device, mesh=mesh, in_specs=in_specs, out_specs=out_specs, check_vma=False)
```

```python
import functools
import math

import jax
import jax.numpy as jnp
from jax import lax
from jax.experimental import pallas as pl
from jax.experimental.pallas import tpu as pltpu
from jax.sharding import PartitionSpec as P


SWEEPS = 15
LEVELS = (SWEEPS + 1).bit_length() - 1
PIECES = 2
VMEM = pl.BlockSpec(memory_space=pltpu.VMEM)
SMEM = pl.BlockSpec(memory_space=pltpu.SMEM)
HBM = pl.BlockSpec(memory_space=pltpu.MemorySpace.HBM)


def limit(mib):
    return pltpu.CompilerParams(vmem_limit_bytes=mib << 20)


def f32(*shape):
    return jax.ShapeDtypeStruct(shape, jnp.float32)


def bf16(*shape):
    return jax.ShapeDtypeStruct(shape, jnp.bfloat16)


def permute(x, axis, offset):
    return lax.ppermute(x, axis, [(i, i ^ offset) for i in range(lax.axis_size(axis))])


def exchange(blocks):
    received = [blocks[0]]
    for k in range(1, len(blocks)):
        received.append(permute(blocks[k], "gy", k))
    return received


def call(kernel, **options):
    def run(*args):
        return pl.pallas_call(kernel, **options)(*args)

    return run


def halves(x):
    high = x.astype(jnp.bfloat16)
    return high, (x - high.astype(jnp.float32)).astype(jnp.bfloat16)


def matmul(left, right):
    dot = functools.partial(jnp.dot, preferred_element_type=jnp.float32)
    rows = left[0].shape[0]
    both = dot(jnp.concatenate(left, axis=0), right[0])
    return both[:rows] + (both[rows:] + dot(left[0], right[1]))


def expand(rows):
    half = rows.shape[1] // 2
    return jnp.concatenate([rows, jnp.concatenate([-rows[:, half:], rows[:, :half]], axis=1)], axis=0)


def times(left, right):
    return matmul(left, [expand(x) for x in right])


def joined(ref, rows, cols):
    return jnp.concatenate([ref[0, rows, cols], ref[1, rows, cols]], axis=1)


def panel_of(owner_ref, dest, groups):
    index = jnp.int32(0)
    for p in range(groups):
        index = jnp.where(owner_ref[p] == dest, jnp.int32(p), index)
    return index


def prepare_kernel(edge, ext, groups, cuts, owner_ref, iti_ref, *refs):
    parts, refs = refs[: len(cuts)], refs[len(cuts) :]
    base_ref, res_ref, res_high, res_low, rss_high, rss_low, rse_high, rse_low, shared_ref, sems = refs
    rows_each = ext // groups
    me = lax.axis_index("gy")
    pending = []

    def fetch(src, dst):
        copy = pltpu.make_async_copy(src, dst, sems.at[len(pending)])
        copy.start()
        pending.append(1)
        return copy

    shared = fetch(iti_ref.at[:, ext:, :], shared_ref)
    blocks, others = [], []
    for k in range(groups):
        start = pl.multiple_of(panel_of(owner_ref, me ^ k, groups) * rows_each, 8)
        rows = pl.ds(k * rows_each, rows_each)
        for c in range(2):
            blocks.append(fetch(iti_ref.at[c, pl.ds(start, rows_each), ext:], res_ref.at[rows, c * edge : (c + 1) * edge]))
            others.append(fetch(iti_ref.at[c, pl.ds(start, rows_each), :ext], base_ref.at[c, rows, :]))
    for (lo, hi), part in zip(cuts, parts):
        others.append(fetch(iti_ref.at[:, ext:, lo:hi], part))
    shared.wait()
    rss_high[...], rss_low[...] = halves(joined(shared_ref, slice(None), slice(ext, None)))
    rse_high[...], rse_low[...] = halves(joined(shared_ref, slice(None), slice(0, ext)))
    for copy in blocks:
        copy.wait()
    res_high[...], res_low[...] = halves(res_ref[...])
    for copy in others:
        copy.wait()


def factor_kernel(edge, ext, rows, qss_ref, base_ref, res_ref, res_high, res_low, rss_high, rss_low, rse_high, rse_low, *refs):
    pow_high, pow_low, cols_high, cols_low, far_high, far_low, out_ref = refs
    qss = halves(joined(qss_ref, slice(None), slice(None)))
    power = halves(times(qss, (rss_high[...], rss_low[...])))
    cols_high[...], cols_low[...] = halves(times(qss, (rse_high[...], rse_low[...])))
    total = res_ref[ext - rows :]
    left = res_high[ext - rows :], res_low[ext - rows :]
    for level in range(LEVELS):
        pow_high[level], pow_low[level] = power
        if level + 1 < LEVELS:
            both = times([jnp.concatenate(pair, axis=0) for pair in zip(power, left)], power)
            power = halves(both[:edge])
            total = total + both[edge:]
        else:
            total = total + times(left, power)
        left = halves(total)
    far_high[...], far_low[...] = left
    cols = cols_high[...], cols_low[...]
    finish(edge, ext, [out_ref], times(left, cols), base_ref, ext - rows)


def finish(edge, ext, out_refs, half, base_ref, start):
    weight = math.sqrt(edge)
    rows = half.shape[0] // len(out_refs)
    for n, out_ref in enumerate(out_refs):
        for c in range(2):
            block = half[n * rows : (n + 1) * rows, c * ext : (c + 1) * ext]
            out_ref[c] = (base_ref[c, start + n * rows : start + (n + 1) * rows, :] + block) * weight


def own_half_kernel(edge, ext, rows, base_ref, res_ref, res_high, res_low, pow_high, pow_low, cols_high, cols_low, *refs):
    high_ref, low_ref, *out_refs = refs
    total = res_ref[: ext - rows]
    left = res_high[: ext - rows], res_low[: ext - rows]
    for level in range(LEVELS):
        total = total + times(left, (pow_high[level], pow_low[level]))
        left = halves(total)
    high_ref[...], low_ref[...] = left
    if out_refs:
        finish(edge, ext, out_refs, times([x[rows:] for x in left], (cols_high[...], cols_low[...])), base_ref, rows)


def mine_kernel(edge, ext, rows, base_ref, high_ref, low_ref, cols_high, cols_low, out_ref):
    half = times((high_ref[:rows], low_ref[:rows]), (cols_high[...], cols_low[...]))
    finish(edge, ext, [out_ref], half, base_ref, 0)


def other_half_kernel(edge, groups, high_ref, low_ref, far_high, far_low, *refs):
    qse_refs, out_refs = refs[:-groups], refs[-groups:]
    weight = math.sqrt(edge)
    rows = far_high.shape[0]
    cols = qse_refs[0].shape[-1]
    qse = sum((joined(x, slice(None), slice(None)) for x in qse_refs[1:]), joined(qse_refs[0], slice(None), slice(None)))
    left = [jnp.concatenate([a[...], b[...]], axis=0) for a, b in ((high_ref, far_high), (low_ref, far_low))]
    half = times(left, halves(qse))
    for k in range(groups):
        for c in range(2):
            out_refs[k][c] = half[k * rows : (k + 1) * rows, c * cols : (c + 1) * cols] * weight


def store(sides, parts, ext, out=None):
    groups = len(sides)
    count = groups * len(parts)
    rows = parts[0][1][0].shape[1]

    def kernel(*refs):
        out_ref, sems = refs[-2:]
        me = lax.axis_index("gy")
        copies = []
        for k in range(groups):
            own = (jnp.max(refs[k][...]) > 0.5).astype(jnp.int32) * ext
            for n, (first, _) in enumerate(parts):
                block = refs[groups + n * groups + k]
                col = pl.multiple_of(own if first is None else ext - own + first, 128)
                for c in range(2):
                    dst = out_ref.at[c, me ^ k, :, pl.ds(col, block.shape[-1])]
                    copy = pltpu.make_async_copy(block.at[c], dst, sems.at[2 * (n * groups + k) + c])
                    copy.start()
                    copies.append(copy)
        for copy in copies:
            copy.wait()

    args = [*sides, *(b for _, blocks in parts for b in blocks)] + ([] if out is None else [out])
    return call(
        kernel,
        out_shape=f32(2, groups, rows, 2 * ext),
        in_specs=[VMEM] * (groups + count) + ([] if out is None else [HBM]),
        out_specs=HBM,
        scratch_shapes=[pltpu.SemaphoreType.DMA((2 * count,))],
        input_output_aliases={} if out is None else {groups + count: 0},
        compiler_params=limit(4),
    )(*args)


def on_device(iti, side, owner):
    ownmap = iti[0, 0]
    edge = ownmap.shape[-1] // 4
    ext = 3 * edge
    groups = lax.axis_size("gy")
    rows_each = ext // groups
    across = lax.axis_size("gx") // 2
    cuts = [(0 * edge, 2 * edge), (2 * edge, 3 * edge)]
    assert len(cuts) == PIECES
    qss = permute(ownmap[:, ext:, ext:], "gx", across)
    *pieces, base, res, res_high, res_low, rss_high, rss_low, rse_high, rse_low = call(
        functools.partial(prepare_kernel, edge, ext, groups, cuts),
        out_shape=[f32(2, edge, hi - lo) for lo, hi in cuts]
        + [f32(2, ext, ext), f32(ext, 2 * edge), bf16(ext, 2 * edge), bf16(ext, 2 * edge)]
        + [bf16(edge, 2 * edge)] * 2
        + [bf16(edge, 2 * ext)] * 2,
        in_specs=[SMEM, HBM],
        out_specs=[VMEM] * (8 + len(cuts)),
        scratch_shapes=[pltpu.VMEM((2, edge, 4 * edge), jnp.float32), pltpu.SemaphoreType.DMA((1 + 4 * groups + len(cuts),))],
        compiler_params=limit(12),
    )(owner[0, 0], ownmap)
    inner = [i for i in range(2 * across) if (i // across ^ i // (across // 2)) & 1]
    first = [(i, i ^ across) for i in inner]
    last = [(i ^ across // 2, i ^ across ^ across // 2) for i in inner]
    early = lax.ppermute(pieces[0], "gx", first)
    pow_high, pow_low, cols_high, cols_low, far_high, far_low, farthest = call(
        functools.partial(factor_kernel, edge, ext, rows_each),
        out_shape=[bf16(LEVELS, edge, 2 * edge)] * 2
        + [bf16(edge, 2 * ext)] * 2
        + [bf16(rows_each, 2 * edge)] * 2
        + [f32(2, rows_each, ext)],
        in_specs=[VMEM] * 9,
        out_specs=[VMEM] * 7,
        compiler_params=limit(16),
    )(qss, base, res, res_high, res_low, rss_high, rss_low, rse_high, rse_low)
    piece, far_high = lax.optimization_barrier((pieces[0], far_high))
    qse = [[early, lax.ppermute(piece, "gx", last)]]
    for piece in pieces[1:]:
        piece, qse[-1] = lax.optimization_barrier((piece, qse[-1]))
        qse.append([permute(piece, "gx", across)])
    high, low, *own = call(
        functools.partial(own_half_kernel, edge, ext, rows_each),
        out_shape=[bf16(ext - rows_each, 2 * edge)] * 2 + [f32(2, rows_each, ext)] * (groups - 2),
        in_specs=[VMEM] * 8,
        out_specs=[VMEM] * groups,
        compiler_params=limit(16),
    )(base, res, res_high, res_low, pow_high, pow_low, cols_high, cols_low)
    mine = call(
        functools.partial(mine_kernel, edge, ext, rows_each),
        out_shape=f32(2, rows_each, ext),
        in_specs=[VMEM] * 5,
        out_specs=VMEM,
        compiler_params=limit(16),
    )(base, high, low, cols_high, cols_low)
    own = [mine, *own, farthest]
    own = exchange(own)
    flag = jnp.full((8, 128), side[0, 0].astype(jnp.float32))
    flag, high = lax.optimization_barrier((flag, high))
    sides = exchange([flag] * groups)
    parts = []
    for (lo, hi), part in zip(cuts, qse):
        blocks = call(
            functools.partial(other_half_kernel, edge, groups),
            out_shape=[f32(2, rows_each, hi - lo)] * groups,
            in_specs=[VMEM] * (4 + len(part)),
            out_specs=[VMEM] * groups,
            compiler_params=limit(12),
        )(high, low, far_high, far_low, *part)
        parts.append((lo, exchange(blocks)))
    out = store(sides, [(None, own), *parts[:-1]], ext)
    out = store(sides, parts[-1:], ext, out)
    return out[None, None]


def solution(mesh):
    in_specs = (P("gx", "gy", None, None, None), P("gx", "gy"), P("gx", "gy", None))
    out_specs = P("gx", "gy", None, None, None, None)
    return jax.shard_map(on_device, mesh=mesh, in_specs=in_specs, out_specs=out_specs, check_vma=False)
```

```python
import functools
import math

import jax
import jax.numpy as jnp
from jax import lax
from jax.experimental import pallas as pl
from jax.experimental.pallas import tpu as pltpu
from jax.sharding import PartitionSpec as P


SWEEPS = 15
LEVELS = (SWEEPS + 1).bit_length() - 1
PIECES = 2
VMEM = pl.BlockSpec(memory_space=pltpu.VMEM)
SMEM = pl.BlockSpec(memory_space=pltpu.SMEM)
HBM = pl.BlockSpec(memory_space=pltpu.MemorySpace.HBM)


def limit(mib):
    return pltpu.CompilerParams(vmem_limit_bytes=mib << 20)


def f32(*shape):
    return jax.ShapeDtypeStruct(shape, jnp.float32)


def bf16(*shape):
    return jax.ShapeDtypeStruct(shape, jnp.bfloat16)


def permute(x, axis, offset):
    return lax.ppermute(x, axis, [(i, i ^ offset) for i in range(lax.axis_size(axis))])


def exchange(blocks):
    received = [blocks[0]]
    for k in range(1, len(blocks)):
        received.append(permute(blocks[k], "gy", k))
    return received


def call(kernel, **options):
    def run(*args):
        return pl.pallas_call(kernel, **options)(*args)

    return run


def halves(x):
    high = x.astype(jnp.bfloat16)
    return high, (x - high.astype(jnp.float32)).astype(jnp.bfloat16)


def matmul(left, right):
    dot = functools.partial(jnp.dot, preferred_element_type=jnp.float32)
    rows = left[0].shape[0]
    both = dot(jnp.concatenate(left, axis=0), right[0])
    return both[:rows] + (both[rows:] + dot(left[0], right[1]))


def expand(rows):
    half = rows.shape[1] // 2
    return jnp.concatenate([rows, jnp.concatenate([-rows[:, half:], rows[:, :half]], axis=1)], axis=0)


def times(left, right):
    return matmul(left, [expand(x) for x in right])


def joined(ref, rows, cols):
    return jnp.concatenate([ref[0, rows, cols], ref[1, rows, cols]], axis=1)


def panel_of(owner_ref, dest, groups):
    index = jnp.int32(0)
    for p in range(groups):
        index = jnp.where(owner_ref[p] == dest, jnp.int32(p), index)
    return index


def corner_kernel(ext, iti_ref, out_ref, sem):
    copy = pltpu.make_async_copy(iti_ref.at[:, ext:, ext:], out_ref, sem)
    copy.start()
    copy.wait()


def prepare_kernel(edge, ext, groups, cuts, owner_ref, iti_ref, *refs):
    parts, refs = refs[: len(cuts)], refs[len(cuts) :]
    base_ref, res_ref, res_high, res_low, rss_high, rss_low, rse_high, rse_low, shared_ref, sems = refs
    rows_each = ext // groups
    me = lax.axis_index("gy")
    pending = []

    def fetch(src, dst):
        copy = pltpu.make_async_copy(src, dst, sems.at[len(pending)])
        copy.start()
        pending.append(1)
        return copy

    shared = fetch(iti_ref.at[:, ext:, :], shared_ref)
    blocks, others = [], []
    for k in range(groups):
        start = pl.multiple_of(panel_of(owner_ref, me ^ k, groups) * rows_each, 8)
        rows = pl.ds(k * rows_each, rows_each)
        for c in range(2):
            blocks.append(fetch(iti_ref.at[c, pl.ds(start, rows_each), ext:], res_ref.at[rows, c * edge : (c + 1) * edge]))
            others.append(fetch(iti_ref.at[c, pl.ds(start, rows_each), :ext], base_ref.at[c, rows, :]))
    for (lo, hi), part in zip(cuts, parts):
        others.append(fetch(iti_ref.at[:, ext:, lo:hi], part))
    shared.wait()
    rss_high[...], rss_low[...] = halves(joined(shared_ref, slice(None), slice(ext, None)))
    rse_high[...], rse_low[...] = halves(joined(shared_ref, slice(None), slice(0, ext)))
    for copy in blocks:
        copy.wait()
    res_high[...], res_low[...] = halves(res_ref[...])
    for copy in others:
        copy.wait()


def factor_kernel(edge, ext, rows, qss_ref, base_ref, res_ref, res_high, res_low, rss_high, rss_low, rse_high, rse_low, *refs):
    pow_high, pow_low, cols_high, cols_low, far_high, far_low, out_ref = refs
    qss = halves(joined(qss_ref, slice(None), slice(None)))
    power = halves(times(qss, (rss_high[...], rss_low[...])))
    cols_high[...], cols_low[...] = halves(times(qss, (rse_high[...], rse_low[...])))
    total = res_ref[ext - rows :]
    left = res_high[ext - rows :], res_low[ext - rows :]
    for level in range(LEVELS):
        pow_high[level], pow_low[level] = power
        if level + 1 < LEVELS:
            both = times([jnp.concatenate(pair, axis=0) for pair in zip(power, left)], power)
            power = halves(both[:edge])
            total = total + both[edge:]
        else:
            total = total + times(left, power)
        left = halves(total)
    far_high[...], far_low[...] = left
    cols = cols_high[...], cols_low[...]
    finish(edge, ext, [out_ref], times(left, cols), base_ref, ext - rows)


def finish(edge, ext, out_refs, half, base_ref, start):
    weight = math.sqrt(edge)
    rows = half.shape[0] // len(out_refs)
    for n, out_ref in enumerate(out_refs):
        for c in range(2):
            block = half[n * rows : (n + 1) * rows, c * ext : (c + 1) * ext]
            out_ref[c] = (base_ref[c, start + n * rows : start + (n + 1) * rows, :] + block) * weight


def own_half_kernel(edge, ext, rows, base_ref, res_ref, res_high, res_low, pow_high, pow_low, cols_high, cols_low, *refs):
    high_ref, low_ref, *out_refs = refs
    total = res_ref[: ext - rows]
    left = res_high[: ext - rows], res_low[: ext - rows]
    for level in range(LEVELS):
        total = total + times(left, (pow_high[level], pow_low[level]))
        left = halves(total)
    high_ref[...], low_ref[...] = left
    if out_refs:
        finish(edge, ext, out_refs, times([x[rows:] for x in left], (cols_high[...], cols_low[...])), base_ref, rows)


def mine_kernel(edge, ext, rows, base_ref, high_ref, low_ref, cols_high, cols_low, out_ref):
    half = times((high_ref[:rows], low_ref[:rows]), (cols_high[...], cols_low[...]))
    finish(edge, ext, [out_ref], half, base_ref, 0)


def other_half_kernel(edge, groups, high_ref, low_ref, far_high, far_low, *refs):
    qse_refs, out_refs = refs[:-groups], refs[-groups:]
    weight = math.sqrt(edge)
    rows = far_high.shape[0]
    cols = qse_refs[0].shape[-1]
    qse = sum((joined(x, slice(None), slice(None)) for x in qse_refs[1:]), joined(qse_refs[0], slice(None), slice(None)))
    left = [jnp.concatenate([a[...], b[...]], axis=0) for a, b in ((high_ref, far_high), (low_ref, far_low))]
    half = times(left, halves(qse))
    for k in range(groups):
        for c in range(2):
            out_refs[k][c] = half[k * rows : (k + 1) * rows, c * cols : (c + 1) * cols] * weight


def store(sides, parts, ext, out=None):
    groups = len(sides)
    count = groups * len(parts)
    rows = parts[0][1][0].shape[1]

    def kernel(*refs):
        out_ref, sems = refs[-2:]
        me = lax.axis_index("gy")
        copies = []
        for k in range(groups):
            own = (jnp.max(refs[k][...]) > 0.5).astype(jnp.int32) * ext
            for n, (first, _) in enumerate(parts):
                block = refs[groups + n * groups + k]
                col = pl.multiple_of(own if first is None else ext - own + first, 128)
                for c in range(2):
                    dst = out_ref.at[c, me ^ k, :, pl.ds(col, block.shape[-1])]
                    copy = pltpu.make_async_copy(block.at[c], dst, sems.at[2 * (n * groups + k) + c])
                    copy.start()
                    copies.append(copy)
        for copy in copies:
            copy.wait()

    args = [*sides, *(b for _, blocks in parts for b in blocks)] + ([] if out is None else [out])
    return call(
        kernel,
        out_shape=f32(2, groups, rows, 2 * ext),
        in_specs=[VMEM] * (groups + count) + ([] if out is None else [HBM]),
        out_specs=HBM,
        scratch_shapes=[pltpu.SemaphoreType.DMA((2 * count,))],
        input_output_aliases={} if out is None else {groups + count: 0},
        compiler_params=limit(4),
    )(*args)


def on_device(iti, side, owner):
    ownmap = iti[0, 0]
    edge = ownmap.shape[-1] // 4
    ext = 3 * edge
    groups = lax.axis_size("gy")
    rows_each = ext // groups
    across = lax.axis_size("gx") // 2
    cuts = [(0 * edge, 2 * edge), (2 * edge, 3 * edge)]
    assert len(cuts) == PIECES
    corner = pl.pallas_call(
        functools.partial(corner_kernel, ext),
        out_shape=f32(2, edge, edge),
        in_specs=[HBM],
        out_specs=VMEM,
        scratch_shapes=[pltpu.SemaphoreType.DMA],
        compiler_params=limit(52),
    )(ownmap)
    qss = permute(corner, "gx", across)
    *pieces, base, res, res_high, res_low, rss_high, rss_low, rse_high, rse_low = call(
        functools.partial(prepare_kernel, edge, ext, groups, cuts),
        out_shape=[f32(2, edge, hi - lo) for lo, hi in cuts]
        + [f32(2, ext, ext), f32(ext, 2 * edge), bf16(ext, 2 * edge), bf16(ext, 2 * edge)]
        + [bf16(edge, 2 * edge)] * 2
        + [bf16(edge, 2 * ext)] * 2,
        in_specs=[SMEM, HBM],
        out_specs=[VMEM] * (8 + len(cuts)),
        scratch_shapes=[pltpu.VMEM((2, edge, 4 * edge), jnp.float32), pltpu.SemaphoreType.DMA((1 + 4 * groups + len(cuts),))],
        compiler_params=limit(12),
    )(owner[0, 0], ownmap)
    inner = [i for i in range(2 * across) if (i // across ^ i // (across // 2)) & 1]
    first = [(i, i ^ across) for i in inner]
    last = [(i ^ across // 2, i ^ across ^ across // 2) for i in inner]
    early = lax.ppermute(pieces[0], "gx", first)
    pow_high, pow_low, cols_high, cols_low, far_high, far_low, farthest = call(
        functools.partial(factor_kernel, edge, ext, rows_each),
        out_shape=[bf16(LEVELS, edge, 2 * edge)] * 2
        + [bf16(edge, 2 * ext)] * 2
        + [bf16(rows_each, 2 * edge)] * 2
        + [f32(2, rows_each, ext)],
        in_specs=[VMEM] * 9,
        out_specs=[VMEM] * 7,
        compiler_params=limit(16),
    )(qss, base, res, res_high, res_low, rss_high, rss_low, rse_high, rse_low)
    piece, far_high = lax.optimization_barrier((pieces[0], far_high))
    qse = [[early, lax.ppermute(piece, "gx", last)]]
    for piece in pieces[1:]:
        piece, far_high = lax.optimization_barrier((piece, far_high))
        qse.append([permute(piece, "gx", across)])
    high, low, *own = call(
        functools.partial(own_half_kernel, edge, ext, rows_each),
        out_shape=[bf16(ext - rows_each, 2 * edge)] * 2 + [f32(2, rows_each, ext)] * (groups - 2),
        in_specs=[VMEM] * 8,
        out_specs=[VMEM] * groups,
        compiler_params=limit(16),
    )(base, res, res_high, res_low, pow_high, pow_low, cols_high, cols_low)
    mine = call(
        functools.partial(mine_kernel, edge, ext, rows_each),
        out_shape=f32(2, rows_each, ext),
        in_specs=[VMEM] * 5,
        out_specs=VMEM,
        compiler_params=limit(16),
    )(base, high, low, cols_high, cols_low)
    own = [mine, *own, farthest]
    own = exchange(own)
    flag = jnp.full((8, 128), side[0, 0].astype(jnp.float32))
    flag, high = lax.optimization_barrier((flag, high))
    sides = exchange([flag] * groups)
    parts = []
    for (lo, hi), part in zip(cuts, qse):
        blocks = call(
            functools.partial(other_half_kernel, edge, groups),
            out_shape=[f32(2, rows_each, hi - lo)] * groups,
            in_specs=[VMEM] * (4 + len(part)),
            out_specs=[VMEM] * groups,
            compiler_params=limit(12),
        )(high, low, far_high, far_low, *part)
        parts.append((lo, exchange(blocks)))
    out = store(sides, [(None, own), *parts[:-1]], ext)
    out = store(sides, parts[-1:], ext, out)
    return out[None, None]


def solution(mesh):
    in_specs = (P("gx", "gy", None, None, None), P("gx", "gy"), P("gx", "gy", None))
    out_specs = P("gx", "gy", None, None, None, None)
    return jax.shard_map(on_device, mesh=mesh, in_specs=in_specs, out_specs=out_specs, check_vma=False)
```

```python
import functools
import math

import jax
import jax.numpy as jnp
from jax import lax
from jax.experimental import pallas as pl
from jax.experimental.pallas import tpu as pltpu
from jax.sharding import PartitionSpec as P


SWEEPS = 15
LEVELS = (SWEEPS + 1).bit_length() - 1
PIECES = 2
VMEM = pl.BlockSpec(memory_space=pltpu.VMEM)
SMEM = pl.BlockSpec(memory_space=pltpu.SMEM)
HBM = pl.BlockSpec(memory_space=pltpu.MemorySpace.HBM)


def limit(mib):
    return pltpu.CompilerParams(vmem_limit_bytes=mib << 20)


def f32(*shape):
    return jax.ShapeDtypeStruct(shape, jnp.float32)


def bf16(*shape):
    return jax.ShapeDtypeStruct(shape, jnp.bfloat16)


def permute(x, axis, offset):
    return lax.ppermute(x, axis, [(i, i ^ offset) for i in range(lax.axis_size(axis))])


def exchange(blocks):
    received = [blocks[0]]
    for k in range(1, len(blocks)):
        received.append(permute(blocks[k], "gy", k))
    return received


def call(kernel, **options):
    def run(*args):
        return pl.pallas_call(kernel, **options)(*args)

    return run


def halves(x):
    high = x.astype(jnp.bfloat16)
    return high, (x - high.astype(jnp.float32)).astype(jnp.bfloat16)


def matmul(left, right):
    dot = functools.partial(jnp.dot, preferred_element_type=jnp.float32)
    rows = left[0].shape[0]
    both = dot(jnp.concatenate(left, axis=0), right[0])
    return both[:rows] + (both[rows:] + dot(left[0], right[1]))


def expand(rows):
    half = rows.shape[1] // 2
    return jnp.concatenate([rows, jnp.concatenate([-rows[:, half:], rows[:, :half]], axis=1)], axis=0)


def times(left, right):
    return matmul(left, [expand(x) for x in right])


def joined(ref, rows, cols):
    return jnp.concatenate([ref[0, rows, cols], ref[1, rows, cols]], axis=1)


def panel_of(owner_ref, dest, groups):
    index = jnp.int32(0)
    for p in range(groups):
        index = jnp.where(owner_ref[p] == dest, jnp.int32(p), index)
    return index


def corner_kernel(ext, iti_ref, out_ref, sem):
    copy = pltpu.make_async_copy(iti_ref.at[:, ext:, ext:], out_ref, sem)
    copy.start()
    copy.wait()


def prepare_kernel(edge, ext, groups, cuts, owner_ref, iti_ref, *refs):
    parts, refs = refs[: len(cuts)], refs[len(cuts) :]
    base_ref, res_ref, res_high, res_low, rss_high, rss_low, rse_high, rse_low, shared_ref, sems = refs
    rows_each = ext // groups
    me = lax.axis_index("gy")
    pending = []

    def fetch(src, dst):
        copy = pltpu.make_async_copy(src, dst, sems.at[len(pending)])
        copy.start()
        pending.append(1)
        return copy

    shared = fetch(iti_ref.at[:, ext:, :], shared_ref)
    blocks, others = [], []
    for k in range(groups):
        start = pl.multiple_of(panel_of(owner_ref, me ^ k, groups) * rows_each, 8)
        rows = pl.ds(k * rows_each, rows_each)
        for c in range(2):
            blocks.append(fetch(iti_ref.at[c, pl.ds(start, rows_each), ext:], res_ref.at[rows, c * edge : (c + 1) * edge]))
            others.append(fetch(iti_ref.at[c, pl.ds(start, rows_each), :ext], base_ref.at[c, rows, :]))
    for (lo, hi), part in zip(cuts, parts):
        others.append(fetch(iti_ref.at[:, ext:, lo:hi], part))
    shared.wait()
    rss_high[...], rss_low[...] = halves(joined(shared_ref, slice(None), slice(ext, None)))
    rse_high[...], rse_low[...] = halves(joined(shared_ref, slice(None), slice(0, ext)))
    for copy in blocks:
        copy.wait()
    res_high[...], res_low[...] = halves(res_ref[...])
    for copy in others:
        copy.wait()


def factor_kernel(edge, ext, rows, qss_ref, base_ref, res_ref, res_high, res_low, rss_high, rss_low, rse_high, rse_low, *refs):
    pow_high, pow_low, cols_high, cols_low, far_high, far_low, out_ref = refs
    qss = halves(joined(qss_ref, slice(None), slice(None)))
    power = halves(times(qss, (rss_high[...], rss_low[...])))
    cols_high[...], cols_low[...] = halves(times(qss, (rse_high[...], rse_low[...])))
    total = res_ref[ext - rows :]
    left = res_high[ext - rows :], res_low[ext - rows :]
    for level in range(LEVELS):
        pow_high[level], pow_low[level] = power
        if level + 1 < LEVELS:
            both = times([jnp.concatenate(pair, axis=0) for pair in zip(power, left)], power)
            power = halves(both[:edge])
            total = total + both[edge:]
        else:
            total = total + times(left, power)
        left = halves(total)
    far_high[...], far_low[...] = left
    cols = cols_high[...], cols_low[...]
    finish(edge, ext, [out_ref], times(left, cols), base_ref, ext - rows)


def finish(edge, ext, out_refs, half, base_ref, start):
    weight = math.sqrt(edge)
    rows = half.shape[0] // len(out_refs)
    for n, out_ref in enumerate(out_refs):
        for c in range(2):
            block = half[n * rows : (n + 1) * rows, c * ext : (c + 1) * ext]
            out_ref[c] = (base_ref[c, start + n * rows : start + (n + 1) * rows, :] + block) * weight


def own_half_kernel(edge, ext, rows, base_ref, res_ref, res_high, res_low, pow_high, pow_low, cols_high, cols_low, *refs):
    high_ref, low_ref, *out_refs = refs
    total = res_ref[: ext - rows]
    left = res_high[: ext - rows], res_low[: ext - rows]
    for level in range(LEVELS):
        total = total + times(left, (pow_high[level], pow_low[level]))
        left = halves(total)
    high_ref[...], low_ref[...] = left
    if out_refs:
        finish(edge, ext, out_refs, times([x[rows:] for x in left], (cols_high[...], cols_low[...])), base_ref, rows)


def mine_kernel(edge, ext, rows, base_ref, high_ref, low_ref, cols_high, cols_low, out_ref):
    half = times((high_ref[:rows], low_ref[:rows]), (cols_high[...], cols_low[...]))
    finish(edge, ext, [out_ref], half, base_ref, 0)


def other_half_kernel(edge, groups, high_ref, low_ref, far_high, far_low, *refs):
    qse_refs, out_refs = refs[:-groups], refs[-groups:]
    weight = math.sqrt(edge)
    rows = far_high.shape[0]
    cols = qse_refs[0].shape[-1]
    qse = sum((joined(x, slice(None), slice(None)) for x in qse_refs[1:]), joined(qse_refs[0], slice(None), slice(None)))
    left = [jnp.concatenate([a[...], b[...]], axis=0) for a, b in ((high_ref, far_high), (low_ref, far_low))]
    half = times(left, halves(qse))
    for k in range(groups):
        for c in range(2):
            out_refs[k][c] = half[k * rows : (k + 1) * rows, c * cols : (c + 1) * cols] * weight


def store(sides, parts, ext, out=None):
    groups = len(sides)
    blocks = [block for _, part in parts for block in part.values()]
    places = [(first, k) for first, part in parts for k in part]
    used = sorted({k for _, k in places})
    rows = blocks[0].shape[1]

    def kernel(*refs):
        out_ref, sems = refs[-2:]
        me = lax.axis_index("gy")
        own = {k: (jnp.max(refs[n][0:1, 0:1]) > 0.5).astype(jnp.int32) * ext for n, k in enumerate(used)}
        copies = []
        for n, (first, k) in enumerate(places):
            block = refs[len(used) + n]
            col = pl.multiple_of(own[k] if first is None else ext - own[k] + first, 128)
            for c in range(2):
                dst = out_ref.at[c, me ^ k, :, pl.ds(col, block.shape[-1])]
                copies.append(pltpu.make_async_copy(block.at[c], dst, sems.at[n, c]))
                copies[-1].start()
        for copy in copies:
            copy.wait()

    args = [*(sides[k] for k in used), *blocks] + ([] if out is None else [out])
    return call(
        kernel,
        out_shape=f32(2, groups, rows, 2 * ext),
        in_specs=[VMEM] * (len(used) + len(blocks)) + ([] if out is None else [HBM]),
        out_specs=HBM,
        scratch_shapes=[pltpu.SemaphoreType.DMA((len(blocks), 2))],
        input_output_aliases={} if out is None else {len(used) + len(blocks): 0},
        compiler_params=limit(4),
    )(*args)


def on_device(iti, side, owner):
    ownmap = iti[0, 0]
    edge = ownmap.shape[-1] // 4
    ext = 3 * edge
    groups = lax.axis_size("gy")
    rows_each = ext // groups
    across = lax.axis_size("gx") // 2
    cuts = [(0 * edge, 2 * edge), (2 * edge, 3 * edge)]
    assert len(cuts) == PIECES
    corner = pl.pallas_call(
        functools.partial(corner_kernel, ext),
        out_shape=f32(2, edge, edge),
        in_specs=[HBM],
        out_specs=VMEM,
        scratch_shapes=[pltpu.SemaphoreType.DMA],
        compiler_params=limit(52),
    )(ownmap)
    qss = permute(corner, "gx", across)
    *pieces, base, res, res_high, res_low, rss_high, rss_low, rse_high, rse_low = call(
        functools.partial(prepare_kernel, edge, ext, groups, cuts),
        out_shape=[f32(2, edge, hi - lo) for lo, hi in cuts]
        + [f32(2, ext, ext), f32(ext, 2 * edge), bf16(ext, 2 * edge), bf16(ext, 2 * edge)]
        + [bf16(edge, 2 * edge)] * 2
        + [bf16(edge, 2 * ext)] * 2,
        in_specs=[SMEM, HBM],
        out_specs=[VMEM] * (8 + len(cuts)),
        scratch_shapes=[pltpu.VMEM((2, edge, 4 * edge), jnp.float32), pltpu.SemaphoreType.DMA((1 + 4 * groups + len(cuts),))],
        compiler_params=limit(12),
    )(owner[0, 0], ownmap)
    inner = [i for i in range(2 * across) if (i // across ^ i // (across // 2)) & 1]
    first = [(i, i ^ across) for i in inner]
    last = [(i ^ across // 2, i ^ across ^ across // 2) for i in inner]
    early = lax.ppermute(pieces[0], "gx", first)
    pow_high, pow_low, cols_high, cols_low, far_high, far_low, farthest = call(
        functools.partial(factor_kernel, edge, ext, rows_each),
        out_shape=[bf16(LEVELS, edge, 2 * edge)] * 2
        + [bf16(edge, 2 * ext)] * 2
        + [bf16(rows_each, 2 * edge)] * 2
        + [f32(2, rows_each, ext)],
        in_specs=[VMEM] * 9,
        out_specs=[VMEM] * 7,
        compiler_params=limit(16),
    )(qss, base, res, res_high, res_low, rss_high, rss_low, rse_high, rse_low)
    piece, far_high = lax.optimization_barrier((pieces[0], far_high))
    qse = [[early, lax.ppermute(piece, "gx", last)]]
    for piece in pieces[1:]:
        piece, far_high = lax.optimization_barrier((piece, far_high))
        qse.append([permute(piece, "gx", across)])
    high, low, *own = call(
        functools.partial(own_half_kernel, edge, ext, rows_each),
        out_shape=[bf16(ext - rows_each, 2 * edge)] * 2 + [f32(2, rows_each, ext)] * (groups - 2),
        in_specs=[VMEM] * 8,
        out_specs=[VMEM] * groups,
        compiler_params=limit(16),
    )(base, res, res_high, res_low, pow_high, pow_low, cols_high, cols_low)
    mine = call(
        functools.partial(mine_kernel, edge, ext, rows_each),
        out_shape=f32(2, rows_each, ext),
        in_specs=[VMEM] * 5,
        out_specs=VMEM,
        compiler_params=limit(16),
    )(base, high, low, cols_high, cols_low)
    own = [mine, *own, farthest]
    own = exchange(own)
    flag = jnp.full((8, 128), side[0, 0].astype(jnp.float32))
    flag, high = lax.optimization_barrier((flag, high))
    sides = exchange([flag] * groups)
    parts = []
    for (lo, hi), part in zip(cuts, qse):
        blocks = call(
            functools.partial(other_half_kernel, edge, groups),
            out_shape=[f32(2, rows_each, hi - lo)] * groups,
            in_specs=[VMEM] * (4 + len(part)),
            out_specs=[VMEM] * groups,
            compiler_params=limit(12),
        )(high, low, far_high, far_low, *part)
        parts.append((lo, exchange(blocks)))
    parts = [(first, dict(enumerate(blocks))) for first, blocks in [(None, own), *parts]]
    first, ahead = parts[-1]
    behind = {k: ahead.pop(k) for k in range(1, groups)}
    out = store(sides, parts, ext)
    out = store(sides, [(first, behind)], ext, out)
    return out[None, None]


def solution(mesh):
    in_specs = (P("gx", "gy", None, None, None), P("gx", "gy"), P("gx", "gy", None))
    out_specs = P("gx", "gy", None, None, None, None)
    return jax.shard_map(on_device, mesh=mesh, in_specs=in_specs, out_specs=out_specs, check_vma=False)
```

```python
import functools
import math

import jax
import jax.numpy as jnp
from jax import lax
from jax.experimental import pallas as pl
from jax.experimental.pallas import tpu as pltpu
from jax.sharding import PartitionSpec as P


SWEEPS = 15
LEVELS = (SWEEPS + 1).bit_length() - 1
PIECES = 2
CUTS = 4
VMEM = pl.BlockSpec(memory_space=pltpu.VMEM)
SMEM = pl.BlockSpec(memory_space=pltpu.SMEM)
HBM = pl.BlockSpec(memory_space=pltpu.MemorySpace.HBM)


def limit(mib):
    return pltpu.CompilerParams(vmem_limit_bytes=mib << 20)


def f32(*shape):
    return jax.ShapeDtypeStruct(shape, jnp.float32)


def bf16(*shape):
    return jax.ShapeDtypeStruct(shape, jnp.bfloat16)


def permute(x, axis, offset):
    return lax.ppermute(x, axis, [(i, i ^ offset) for i in range(lax.axis_size(axis))])


def exchange(blocks):
    received = [blocks[0]]
    for k in range(1, len(blocks)):
        received.append(permute(blocks[k], "gy", k))
    return received


def call(kernel, **options):
    def run(*args):
        return pl.pallas_call(kernel, **options)(*args)

    return run


def halves(x):
    high = x.astype(jnp.bfloat16)
    return high, (x - high.astype(jnp.float32)).astype(jnp.bfloat16)


dot = functools.partial(jnp.dot, preferred_element_type=jnp.float32)


def matmul(left, right):
    rows = left[0].shape[0]
    both = dot(jnp.concatenate(left, axis=0), right[0])
    return both[:rows] + (both[rows:] + dot(left[0], right[1]))


def expand(rows):
    half = rows.shape[1] // 2
    return jnp.concatenate([rows, jnp.concatenate([-rows[:, half:], rows[:, :half]], axis=1)], axis=0)


def times(left, right):
    return matmul(left, [expand(x) for x in right])


def joined(ref, rows, cols):
    return jnp.concatenate([ref[0, rows, cols], ref[1, rows, cols]], axis=1)


def panel_of(owner_ref, dest, groups):
    index = jnp.int32(0)
    for p in range(groups):
        index = jnp.where(owner_ref[p] == dest, jnp.int32(p), index)
    return index


def corner_kernel(ext, iti_ref, out_ref, sems):
    step = out_ref.shape[1] // CUTS
    copies = []
    for c in range(2):
        for n in range(CUTS):
            rows = pl.ds(n * step, step)
            src = iti_ref.at[c, pl.ds(ext + n * step, step), ext:]
            copies.append(pltpu.make_async_copy(src, out_ref.at[c, rows, :], sems.at[c, n]))
            copies[-1].start()
    for copy in copies:
        copy.wait()


def prepare_kernel(edge, ext, groups, cuts, owner_ref, iti_ref, *refs):
    parts, refs = refs[: len(cuts)], refs[len(cuts) :]
    base_ref, res_ref, res_high, res_low, rss_high, rss_low, rse_high, rse_low, shared_ref, sems = refs
    rows_each = ext // groups
    me = lax.axis_index("gy")
    pending = []

    def fetch(src, dst):
        copy = pltpu.make_async_copy(src, dst, sems.at[len(pending)])
        copy.start()
        pending.append(1)
        return copy

    shared = fetch(iti_ref.at[:, ext:, :], shared_ref)
    blocks, others = [], []
    for k in range(groups):
        start = pl.multiple_of(panel_of(owner_ref, me ^ k, groups) * rows_each, 8)
        rows = pl.ds(k * rows_each, rows_each)
        for c in range(2):
            blocks.append(fetch(iti_ref.at[c, pl.ds(start, rows_each), ext:], res_ref.at[rows, c * edge : (c + 1) * edge]))
            others.append(fetch(iti_ref.at[c, pl.ds(start, rows_each), :ext], base_ref.at[c, rows, :]))
    for (lo, hi), part in zip(cuts, parts):
        others.append(fetch(iti_ref.at[:, ext:, lo:hi], part))
    shared.wait()
    rss_high[...], rss_low[...] = halves(joined(shared_ref, slice(None), slice(ext, None)))
    rse_high[...], rse_low[...] = halves(joined(shared_ref, slice(None), slice(0, ext)))
    for copy in blocks:
        copy.wait()
    res_high[...], res_low[...] = halves(res_ref[...])
    for copy in others:
        copy.wait()


def factor_kernel(edge, ext, rows, qss_ref, base_ref, res_ref, res_high, res_low, rss_high, rss_low, rse_high, rse_low, *refs):
    pow_high, pow_low, cols_high, cols_low, far_high, far_low, out_ref = refs
    qss = halves(joined(qss_ref, slice(None), slice(None)))
    power = halves(times(qss, (rss_high[...], rss_low[...])))
    cols_high[...], cols_low[...] = halves(times(qss, (rse_high[...], rse_low[...])))
    total = res_ref[ext - rows :]
    left = res_high[ext - rows :], res_low[ext - rows :]
    for level in range(LEVELS):
        pow_high[level], pow_low[level] = power
        if level + 1 < LEVELS:
            right = [expand(x) for x in power]
            high = dot(jnp.concatenate([*power, *left], axis=0), right[0])
            low = dot(jnp.concatenate([power[0], left[0]], axis=0), right[1])
            power = halves(high[:edge] + (high[edge : 2 * edge] + low[:edge]))
            high = high[2 * edge :]
            total = total + (high[:rows] + (high[rows:] + low[edge:]))
        else:
            total = total + times(left, power)
        left = halves(total)
    far_high[...], far_low[...] = left
    cols = cols_high[...], cols_low[...]
    finish(edge, ext, [out_ref], times(left, cols), base_ref, ext - rows)


def finish(edge, ext, out_refs, half, base_ref, start):
    weight = math.sqrt(edge)
    rows = half.shape[0] // len(out_refs)
    for n, out_ref in enumerate(out_refs):
        for c in range(2):
            block = half[n * rows : (n + 1) * rows, c * ext : (c + 1) * ext]
            out_ref[c] = (base_ref[c, start + n * rows : start + (n + 1) * rows, :] + block) * weight


def own_half_kernel(edge, ext, rows, base_ref, res_ref, res_high, res_low, pow_high, pow_low, cols_high, cols_low, *refs):
    high_ref, low_ref, *out_refs = refs
    total = res_ref[: ext - rows]
    left = res_high[: ext - rows], res_low[: ext - rows]
    for level in range(LEVELS):
        total = total + times(left, (pow_high[level], pow_low[level]))
        left = halves(total)
    high_ref[...], low_ref[...] = left
    if out_refs:
        finish(edge, ext, out_refs, times([x[rows:] for x in left], (cols_high[...], cols_low[...])), base_ref, rows)


def mine_kernel(edge, ext, rows, base_ref, high_ref, low_ref, cols_high, cols_low, out_ref):
    half = times((high_ref[:rows], low_ref[:rows]), (cols_high[...], cols_low[...]))
    finish(edge, ext, [out_ref], half, base_ref, 0)


def other_half_kernel(edge, groups, high_ref, low_ref, far_high, far_low, *refs):
    qse_refs, out_refs = refs[:-groups], refs[-groups:]
    weight = math.sqrt(edge)
    rows = far_high.shape[0]
    cols = qse_refs[0].shape[-1]
    qse = sum((joined(x, slice(None), slice(None)) for x in qse_refs[1:]), joined(qse_refs[0], slice(None), slice(None)))
    left = [jnp.concatenate([a[...], b[...]], axis=0) for a, b in ((high_ref, far_high), (low_ref, far_low))]
    half = times(left, halves(qse))
    for k in range(groups):
        for c in range(2):
            out_refs[k][c] = half[k * rows : (k + 1) * rows, c * cols : (c + 1) * cols] * weight


def store(sides, parts, ext, out=None):
    groups = len(sides)
    blocks = [block for _, part in parts for block in part.values()]
    places = [(first, k) for first, part in parts for k in part]
    used = sorted({k for _, k in places})
    rows = blocks[0].shape[1]

    def kernel(*refs):
        out_ref, sems = refs[-2:]
        me = lax.axis_index("gy")
        own = {k: (jnp.max(refs[n][0:1, 0:1]) > 0.5).astype(jnp.int32) * ext for n, k in enumerate(used)}
        copies = []
        for n, (first, k) in enumerate(places):
            block = refs[len(used) + n]
            col = pl.multiple_of(own[k] if first is None else ext - own[k] + first, 128)
            for c in range(2):
                dst = out_ref.at[c, me ^ k, :, pl.ds(col, block.shape[-1])]
                copies.append(pltpu.make_async_copy(block.at[c], dst, sems.at[n, c]))
                copies[-1].start()
        for copy in copies:
            copy.wait()

    args = [*(sides[k] for k in used), *blocks] + ([] if out is None else [out])
    return call(
        kernel,
        out_shape=f32(2, groups, rows, 2 * ext),
        in_specs=[VMEM] * (len(used) + len(blocks)) + ([] if out is None else [HBM]),
        out_specs=HBM,
        scratch_shapes=[pltpu.SemaphoreType.DMA((len(blocks), 2))],
        input_output_aliases={} if out is None else {len(used) + len(blocks): 0},
        compiler_params=limit(4),
    )(*args)


def on_device(iti, side, owner):
    ownmap = iti[0, 0]
    edge = ownmap.shape[-1] // 4
    ext = 3 * edge
    groups = lax.axis_size("gy")
    rows_each = ext // groups
    across = lax.axis_size("gx") // 2
    cuts = [(0 * edge, 2 * edge), (2 * edge, 3 * edge)]
    assert len(cuts) == PIECES
    corner = pl.pallas_call(
        functools.partial(corner_kernel, ext),
        out_shape=f32(2, edge, edge),
        in_specs=[HBM],
        out_specs=VMEM,
        scratch_shapes=[pltpu.SemaphoreType.DMA((2, CUTS))],
        compiler_params=limit(52),
    )(ownmap)
    qss = permute(corner, "gx", across)
    *pieces, base, res, res_high, res_low, rss_high, rss_low, rse_high, rse_low = call(
        functools.partial(prepare_kernel, edge, ext, groups, cuts),
        out_shape=[f32(2, edge, hi - lo) for lo, hi in cuts]
        + [f32(2, ext, ext), f32(ext, 2 * edge), bf16(ext, 2 * edge), bf16(ext, 2 * edge)]
        + [bf16(edge, 2 * edge)] * 2
        + [bf16(edge, 2 * ext)] * 2,
        in_specs=[SMEM, HBM],
        out_specs=[VMEM] * (8 + len(cuts)),
        scratch_shapes=[pltpu.VMEM((2, edge, 4 * edge), jnp.float32), pltpu.SemaphoreType.DMA((1 + 4 * groups + len(cuts),))],
        compiler_params=limit(50),
    )(owner[0, 0], ownmap)
    inner = [i for i in range(2 * across) if (i // across ^ i // (across // 2)) & 1]
    first = [(i, i ^ across) for i in inner]
    last = [(i ^ across // 2, i ^ across ^ across // 2) for i in inner]
    early = lax.ppermute(pieces[0], "gx", first)
    pow_high, pow_low, cols_high, cols_low, far_high, far_low, farthest = call(
        functools.partial(factor_kernel, edge, ext, rows_each),
        out_shape=[bf16(LEVELS, edge, 2 * edge)] * 2
        + [bf16(edge, 2 * ext)] * 2
        + [bf16(rows_each, 2 * edge)] * 2
        + [f32(2, rows_each, ext)],
        in_specs=[VMEM] * 9,
        out_specs=[VMEM] * 7,
        compiler_params=pltpu.CompilerParams(vmem_limit_bytes=16 << 20),
    )(qss, base, res, res_high, res_low, rss_high, rss_low, rse_high, rse_low)
    piece, far_high = lax.optimization_barrier((pieces[0], far_high))
    qse = [[early, lax.ppermute(piece, "gx", last)]]
    for piece in pieces[1:]:
        piece, far_high = lax.optimization_barrier((piece, far_high))
        qse.append([permute(piece, "gx", across)])
    high, low, *own = call(
        functools.partial(own_half_kernel, edge, ext, rows_each),
        out_shape=[bf16(ext - rows_each, 2 * edge)] * 2 + [f32(2, rows_each, ext)] * (groups - 2),
        in_specs=[VMEM] * 8,
        out_specs=[VMEM] * groups,
        compiler_params=limit(16),
    )(base, res, res_high, res_low, pow_high, pow_low, cols_high, cols_low)
    mine = call(
        functools.partial(mine_kernel, edge, ext, rows_each),
        out_shape=f32(2, rows_each, ext),
        in_specs=[VMEM] * 5,
        out_specs=VMEM,
        compiler_params=limit(16),
    )(base, high, low, cols_high, cols_low)
    own = [mine, *own, farthest]
    own = exchange(own)
    flag = jnp.full((8, 128), side[0, 0].astype(jnp.float32))
    flag, high = lax.optimization_barrier((flag, high))
    sides = exchange([flag] * groups)
    parts = []
    for (lo, hi), part in zip(cuts, qse):
        blocks = call(
            functools.partial(other_half_kernel, edge, groups),
            out_shape=[f32(2, rows_each, hi - lo)] * groups,
            in_specs=[VMEM] * (4 + len(part)),
            out_specs=[VMEM] * groups,
            compiler_params=limit(12),
        )(high, low, far_high, far_low, *part)
        parts.append((lo, exchange(blocks)))
    parts = [(first, dict(enumerate(blocks))) for first, blocks in [(None, own), *parts]]
    first, ahead = parts[-1]
    behind = {k: ahead.pop(k) for k in range(1, groups)}
    out = store(sides, parts, ext)
    out = store(sides, [(first, behind)], ext, out)
    return out[None, None]


def solution(mesh):
    in_specs = (P("gx", "gy", None, None, None), P("gx", "gy"), P("gx", "gy", None))
    out_specs = P("gx", "gy", None, None, None, None)
    return jax.shard_map(on_device, mesh=mesh, in_specs=in_specs, out_specs=out_specs, check_vma=False)
```

```python
import functools
import math

import jax
import jax.numpy as jnp
from jax import lax
from jax.experimental import pallas as pl
from jax.experimental.pallas import tpu as pltpu
from jax.sharding import PartitionSpec as P


SWEEPS = 15
LEVELS = (SWEEPS + 1).bit_length() - 1
PIECES = 2
CUTS = 4
VMEM = pl.BlockSpec(memory_space=pltpu.VMEM)
SMEM = pl.BlockSpec(memory_space=pltpu.SMEM)
HBM = pl.BlockSpec(memory_space=pltpu.MemorySpace.HBM)


def limit(mib):
    return pltpu.CompilerParams(vmem_limit_bytes=mib << 20)


def f32(*shape):
    return jax.ShapeDtypeStruct(shape, jnp.float32)


def bf16(*shape):
    return jax.ShapeDtypeStruct(shape, jnp.bfloat16)


def permute(x, axis, offset):
    return lax.ppermute(x, axis, [(i, i ^ offset) for i in range(lax.axis_size(axis))])


def exchange(blocks):
    received = [blocks[0]]
    for k in range(1, len(blocks)):
        received.append(permute(blocks[k], "gy", k))
    return received


def call(kernel, **options):
    def run(*args):
        return pl.pallas_call(kernel, **options)(*args)

    return run


def halves(x):
    high = x.astype(jnp.bfloat16)
    return high, (x - high.astype(jnp.float32)).astype(jnp.bfloat16)


def matmul(left, right):
    dot = functools.partial(jnp.dot, preferred_element_type=jnp.float32)
    rows = left[0].shape[0]
    both = dot(jnp.concatenate(left, axis=0), right[0])
    return both[:rows] + (both[rows:] + dot(left[0], right[1]))


def expand(rows):
    half = rows.shape[1] // 2
    return jnp.concatenate([rows, jnp.concatenate([-rows[:, half:], rows[:, :half]], axis=1)], axis=0)


def times(left, right):
    return matmul(left, [expand(x) for x in right])


def joined(ref, rows, cols):
    return jnp.concatenate([ref[0, rows, cols], ref[1, rows, cols]], axis=1)


def panel_of(owner_ref, dest, groups):
    index = jnp.int32(0)
    for p in range(groups):
        index = jnp.where(owner_ref[p] == dest, jnp.int32(p), index)
    return index


def corner_kernel(ext, iti_ref, out_ref, sems):
    step = out_ref.shape[1] // CUTS
    copies = []
    for c in range(2):
        for n in range(CUTS):
            rows = pl.ds(n * step, step)
            src = iti_ref.at[c, pl.ds(ext + n * step, step), ext:]
            copies.append(pltpu.make_async_copy(src, out_ref.at[c, rows, :], sems.at[c, n]))
            copies[-1].start()
    for copy in copies:
        copy.wait()


def prepare_kernel(edge, ext, groups, cuts, owner_ref, iti_ref, *refs):
    parts, refs = refs[: len(cuts)], refs[len(cuts) :]
    base_ref, res_ref, res_high, res_low, rss_high, rss_low, rse_high, rse_low, shared_ref, sems = refs
    rows_each = ext // groups
    me = lax.axis_index("gy")
    pending = []

    def fetch(src, dst):
        copy = pltpu.make_async_copy(src, dst, sems.at[len(pending)])
        copy.start()
        pending.append(1)
        return copy

    shared = fetch(iti_ref.at[:, ext:, :], shared_ref)
    blocks, others = [], []
    for k in range(groups):
        start = pl.multiple_of(panel_of(owner_ref, me ^ k, groups) * rows_each, 8)
        rows = pl.ds(k * rows_each, rows_each)
        for c in range(2):
            blocks.append(fetch(iti_ref.at[c, pl.ds(start, rows_each), ext:], res_ref.at[rows, c * edge : (c + 1) * edge]))
            others.append(fetch(iti_ref.at[c, pl.ds(start, rows_each), :ext], base_ref.at[c, rows, :]))
    for (lo, hi), part in zip(cuts, parts):
        others.append(fetch(iti_ref.at[:, ext:, lo:hi], part))
    shared.wait()
    rss_high[...], rss_low[...] = halves(joined(shared_ref, slice(None), slice(ext, None)))
    rse_high[...], rse_low[...] = halves(joined(shared_ref, slice(None), slice(0, ext)))
    for copy in blocks:
        copy.wait()
    res_high[...], res_low[...] = halves(res_ref[...])
    for copy in others:
        copy.wait()


def factor_kernel(edge, ext, rows, qss_ref, base_ref, res_ref, res_high, res_low, rss_high, rss_low, rse_high, rse_low, *refs):
    pow_high, pow_low, cols_high, cols_low, far_high, far_low, out_ref = refs
    qss = halves(joined(qss_ref, slice(None), slice(None)))
    power = halves(times(qss, (rss_high[...], rss_low[...])))
    cols_high[...], cols_low[...] = halves(times(qss, (rse_high[...], rse_low[...])))
    total = res_ref[ext - rows :]
    left = res_high[ext - rows :], res_low[ext - rows :]
    for level in range(LEVELS):
        pow_high[level], pow_low[level] = power
        if level + 1 < LEVELS:
            both = times([jnp.concatenate(pair, axis=0) for pair in zip(power, left)], power)
            power = halves(both[:edge])
            total = total + both[edge:]
        else:
            total = total + times(left, power)
        left = halves(total)
    far_high[...], far_low[...] = left
    cols = cols_high[...], cols_low[...]
    finish(edge, ext, [out_ref], times(left, cols), base_ref, ext - rows)


def finish(edge, ext, out_refs, half, base_ref, start):
    weight = math.sqrt(edge)
    rows = half.shape[0] // len(out_refs)
    for n, out_ref in enumerate(out_refs):
        for c in range(2):
            block = half[n * rows : (n + 1) * rows, c * ext : (c + 1) * ext]
            out_ref[c] = (base_ref[c, start + n * rows : start + (n + 1) * rows, :] + block) * weight


def own_half_kernel(edge, ext, rows, base_ref, res_ref, res_high, res_low, pow_high, pow_low, cols_high, cols_low, *refs):
    high_ref, low_ref, *out_refs = refs
    total = res_ref[: ext - rows]
    left = res_high[: ext - rows], res_low[: ext - rows]
    for level in range(LEVELS):
        total = total + times(left, (pow_high[level], pow_low[level]))
        left = halves(total)
    high_ref[...], low_ref[...] = left
    if out_refs:
        finish(edge, ext, out_refs, times([x[rows:] for x in left], (cols_high[...], cols_low[...])), base_ref, rows)


def mine_kernel(edge, ext, rows, base_ref, high_ref, low_ref, cols_high, cols_low, out_ref):
    half = times((high_ref[:rows], low_ref[:rows]), (cols_high[...], cols_low[...]))
    finish(edge, ext, [out_ref], half, base_ref, 0)


def other_half_kernel(edge, groups, high_ref, low_ref, far_high, far_low, *refs):
    qse_refs, out_refs = refs[:-groups], refs[-groups:]
    weight = math.sqrt(edge)
    rows = far_high.shape[0]
    cols = qse_refs[0].shape[-1]
    qse = sum((joined(x, slice(None), slice(None)) for x in qse_refs[1:]), joined(qse_refs[0], slice(None), slice(None)))
    left = [jnp.concatenate([a[...], b[...]], axis=0) for a, b in ((high_ref, far_high), (low_ref, far_low))]
    half = times(left, halves(qse))
    for k in range(groups):
        for c in range(2):
            out_refs[k][c] = half[k * rows : (k + 1) * rows, c * cols : (c + 1) * cols] * weight


def store(sides, parts, ext, out=None):
    groups = len(sides)
    blocks = [block for _, part in parts for block in part.values()]
    places = [(first, k) for first, part in parts for k in part]
    used = sorted({k for _, k in places})
    rows = blocks[0].shape[1]

    def kernel(*refs):
        out_ref, sems = refs[-2:]
        me = lax.axis_index("gy")
        own = {k: (jnp.max(refs[n][0:1, 0:1]) > 0.5).astype(jnp.int32) * ext for n, k in enumerate(used)}
        copies = []
        for n, (first, k) in enumerate(places):
            block = refs[len(used) + n]
            col = pl.multiple_of(own[k] if first is None else ext - own[k] + first, 128)
            for c in range(2):
                dst = out_ref.at[c, me ^ k, :, pl.ds(col, block.shape[-1])]
                copies.append(pltpu.make_async_copy(block.at[c], dst, sems.at[n, c]))
                copies[-1].start()
        for copy in copies:
            copy.wait()

    args = [*(sides[k] for k in used), *blocks] + ([] if out is None else [out])
    return call(
        kernel,
        out_shape=f32(2, groups, rows, 2 * ext),
        in_specs=[VMEM] * (len(used) + len(blocks)) + ([] if out is None else [HBM]),
        out_specs=HBM,
        scratch_shapes=[pltpu.SemaphoreType.DMA((len(blocks), 2))],
        input_output_aliases={} if out is None else {len(used) + len(blocks): 0},
        compiler_params=limit(4),
    )(*args)


def on_device(iti, side, owner):
    ownmap = iti[0, 0]
    edge = ownmap.shape[-1] // 4
    ext = 3 * edge
    groups = lax.axis_size("gy")
    rows_each = ext // groups
    across = lax.axis_size("gx") // 2
    cuts = [(0 * edge, 2 * edge), (2 * edge, 3 * edge)]
    assert len(cuts) == PIECES
    corner = pl.pallas_call(
        functools.partial(corner_kernel, ext),
        out_shape=f32(2, edge, edge),
        in_specs=[HBM],
        out_specs=VMEM,
        scratch_shapes=[pltpu.SemaphoreType.DMA((2, CUTS))],
        compiler_params=limit(52),
    )(ownmap)
    qss = permute(corner, "gx", across)
    *pieces, base, res, res_high, res_low, rss_high, rss_low, rse_high, rse_low = call(
        functools.partial(prepare_kernel, edge, ext, groups, cuts),
        out_shape=[f32(2, edge, hi - lo) for lo, hi in cuts]
        + [f32(2, ext, ext), f32(ext, 2 * edge), bf16(ext, 2 * edge), bf16(ext, 2 * edge)]
        + [bf16(edge, 2 * edge)] * 2
        + [bf16(edge, 2 * ext)] * 2,
        in_specs=[SMEM, HBM],
        out_specs=[VMEM] * (8 + len(cuts)),
        scratch_shapes=[pltpu.VMEM((2, edge, 4 * edge), jnp.float32), pltpu.SemaphoreType.DMA((1 + 4 * groups + len(cuts),))],
        compiler_params=limit(50),
    )(owner[0, 0], ownmap)
    inner = [i for i in range(2 * across) if (i // across ^ i // (across // 2)) & 1]
    first = [(i, i ^ across) for i in inner]
    last = [(i ^ across // 2, i ^ across ^ across // 2) for i in inner]
    early = lax.ppermute(pieces[0], "gx", first)
    pow_high, pow_low, cols_high, cols_low, far_high, far_low, farthest = call(
        functools.partial(factor_kernel, edge, ext, rows_each),
        out_shape=[bf16(LEVELS, edge, 2 * edge)] * 2
        + [bf16(edge, 2 * ext)] * 2
        + [bf16(rows_each, 2 * edge)] * 2
        + [f32(2, rows_each, ext)],
        in_specs=[VMEM] * 9,
        out_specs=[VMEM] * 7,
        compiler_params=pltpu.CompilerParams(vmem_limit_bytes=16 << 20),
    )(qss, base, res, res_high, res_low, rss_high, rss_low, rse_high, rse_low)
    piece, far_high = lax.optimization_barrier((pieces[0], far_high))
    qse = [[early, lax.ppermute(piece, "gx", last)]]
    for piece in pieces[1:]:
        piece, far_high = lax.optimization_barrier((piece, far_high))
        qse.append([permute(piece, "gx", across)])
    high, low, *own = call(
        functools.partial(own_half_kernel, edge, ext, rows_each),
        out_shape=[bf16(ext - rows_each, 2 * edge)] * 2 + [f32(2, rows_each, ext)] * (groups - 2),
        in_specs=[VMEM] * 8,
        out_specs=[VMEM] * groups,
        compiler_params=limit(16),
    )(base, res, res_high, res_low, pow_high, pow_low, cols_high, cols_low)
    mine = call(
        functools.partial(mine_kernel, edge, ext, rows_each),
        out_shape=f32(2, rows_each, ext),
        in_specs=[VMEM] * 5,
        out_specs=VMEM,
        compiler_params=limit(16),
    )(base, high, low, cols_high, cols_low)
    own = [mine, *own, farthest]
    own = exchange(own)
    flag = jnp.full((8, 128), side[0, 0].astype(jnp.float32))
    flag, high = lax.optimization_barrier((flag, high))
    sides = exchange([flag] * groups)
    parts = []
    for (lo, hi), part in zip(cuts, qse):
        blocks = call(
            functools.partial(other_half_kernel, edge, groups),
            out_shape=[f32(2, rows_each, hi - lo)] * groups,
            in_specs=[VMEM] * (4 + len(part)),
            out_specs=[VMEM] * groups,
            compiler_params=limit(12),
        )(high, low, far_high, far_low, *part)
        parts.append((lo, exchange(blocks)))
    parts = [(first, dict(enumerate(blocks))) for first, blocks in [(None, own), *parts]]
    first, ahead = parts[-1]
    behind = {k: ahead.pop(k) for k in range(1, groups)}
    out = store(sides, parts, ext)
    out = store(sides, [(first, behind)], ext, out)
    return out[None, None]


def solution(mesh):
    in_specs = (P("gx", "gy", None, None, None), P("gx", "gy"), P("gx", "gy", None))
    out_specs = P("gx", "gy", None, None, None, None)
    return jax.shard_map(on_device, mesh=mesh, in_specs=in_specs, out_specs=out_specs, check_vma=False)
```
